128 devices in a mesh: gx: 16 (over x, z), gy: 8 (over y, core).
Axes of the slice: x: 4, y: 4, z: 4, core: 2. Of those that a mesh axis runs over, the one named last changes fastest.
Arguments:
- geometry: float32 [8, 524288], P(None, ('gx', 'gy')), may hold values from -1 to 17, as said below
- panel: bfloat16 [524288, 128], P(('gx', 'gy')), may hold values from -6 to 6
- pair_first: int32 [8192], P(('gx', 'gy')), may hold values from 0 to 7
- pair_second: int32 [8192], P(('gx', 'gy')), may hold values from 0 to 71, as said below
- pair_count: int32 [128], P(('gx', 'gy')), may hold values from 1 to 64, as said below
Outputs:
- near_product: float32 [524288, 128], P(('gx', 'gy'))
The draws below stay inside these ranges and needn't reach their ends.
Inputs may be any that keep to these rules, and one draw needn't show every extreme that they name: `geometry`: rows are x, y, z, the unit direction's three components, the length and the radius; lengths lie in 0.25 to 4, radii in 0.005 to 0.02, and a filament of the device at (ix, iy) has x in ix - 0.5 to ix + 1.5 and y in iy - 0.5 to iy + 1.5. `pair_second`: the device named by every slot lies inside the grid of devices; slots at or beyond a device's count hold arbitrary entries of the same form; pairs may repeat. `pair_count`: some device uses all 64 slots.
All inputs are finite; a program needn't handle non-finite values.
Results may differ from the reference program's by a relative error of at most 0.0032.
Values may be sent and summed in bfloat16 or wider, within the bound.
No kernel may reach another device: no remote copies, remote signals or barrier semaphores. Data moves between devices by JAX's collectives and lax.ppermute only.
A program may use at most 128 MiB of HBM per device.

```python
import math
import jax
import jax.numpy as jnp
from jax import lax

BLOCK = 512
COLS = 128
GROUP = 8
BLK_DEV = 8
PAIR_DEV = 64
GRID_X = 16
GRID_Y = 8
FIL_DEV = 4096
FILAMENTS = 524288
PAIRS = 8192


def draw_geometry(key, part):
    subkeys = jax.random.split(key, 7)
    device_ids = jnp.arange(FILAMENTS, dtype=jnp.int32) // FIL_DEV
    dev_x = (device_ids // GRID_Y).astype(jnp.float32)
    dev_y = (device_ids % GRID_Y).astype(jnp.float32)
    draw_shape = (FILAMENTS,)
    height = 1.0
    tilt_range = 1.0
    turn_range = math.pi
    lo_len = 0.5
    hi_len = 2.0
    pos_x = dev_x + jax.random.uniform(subkeys[0], draw_shape, jnp.float32, -0.5, 1.5)
    pos_y = dev_y + jax.random.uniform(subkeys[1], draw_shape, jnp.float32, -0.5, 1.5)
    pos_z = jax.random.uniform(subkeys[2], draw_shape, jnp.float32, 0.0, height)
    lift_cos = jax.random.uniform(subkeys[3], draw_shape, jnp.float32, -tilt_range, tilt_range)
    turn_angle = jax.random.uniform(subkeys[4], draw_shape, jnp.float32, -turn_range, turn_range)
    across = jnp.sqrt(1.0 - lift_cos * lift_cos)
    dir_x = across * jnp.cos(turn_angle)
    dir_y = across * jnp.sin(turn_angle)
    length = jnp.exp(jax.random.uniform(subkeys[5], draw_shape, jnp.float32, math.log(lo_len), math.log(hi_len)))
    radius = jnp.exp(jax.random.uniform(subkeys[6], draw_shape, jnp.float32, math.log(0.005), math.log(0.02)))
    return jnp.stack([pos_x, pos_y, pos_z, dir_x, dir_y, lift_cos, length, radius]).astype(jnp.float32)


def draw_pair_second(key, part):
    subkeys = jax.random.split(key, 2)
    device_ids = jnp.arange(PAIRS, dtype=jnp.int32) // PAIR_DEV
    dev_x = device_ids // GRID_Y
    dev_y = device_ids % GRID_Y
    slot_ids = jax.random.randint(subkeys[0], (PAIRS,), 0, 9, dtype=jnp.int32)
    step_x = slot_ids // 3 - 1
    step_y = slot_ids % 3 - 1
    inside = (dev_x + step_x >= 0) & (dev_x + step_x < GRID_X) & (dev_y + step_y >= 0) & (dev_y + step_y < GRID_Y)
    slot_ids = jnp.where(inside, slot_ids, 4)
    block_ids = jax.random.randint(subkeys[1], (PAIRS,), 0, BLK_DEV, dtype=jnp.int32)
    return (slot_ids * BLK_DEV + block_ids).astype(jnp.int32)


def draw_pair_count(key, part):
    subkeys = jax.random.split(key, 2)
    device_total = GRID_X * GRID_Y
    spread_ids = jax.random.randint(subkeys[0], (device_total,), 0, 64, dtype=jnp.int32)
    counts = 1 + spread_ids * spread_ids * (PAIR_DEV - 1) // 3969
    busiest = jax.random.randint(subkeys[1], (), 0, device_total, dtype=jnp.int32)
    counts = jnp.where(jnp.arange(device_total, dtype=jnp.int32) == busiest, PAIR_DEV, counts)
    return counts.astype(jnp.int32)


def touch_ends(result, stream_key, least, high):
    index_at = [jax.random.randint(jax.random.fold_in(stream_key, axis), (), 0, length) for axis, length in enumerate(result.shape)]
    longest = result.shape.index(max(result.shape))
    beside = index_at[:longest] + [(index_at[longest] + 1) % result.shape[longest]] + index_at[longest + 1:]
    return result.at[tuple(index_at)].set(least).at[tuple(beside)].set(high)


def shard_levels(own_key, dims, cuts, least, high):
    def one(position, blocks):
        heights = jax.random.uniform(jax.random.fold_in(jax.random.fold_in(own_key, 6), position), (blocks,), jnp.float32, least / len(cuts), high / len(cuts))
        return jnp.repeat(jnp.exp(heights), dims[position] // blocks).reshape((-1,) + (1,) * (len(dims) - position - 1))

    factor_of = one(*cuts[0])
    for cut in cuts[1:]:
        factor_of = factor_of * one(*cut)
    return factor_of


def centred(key, dims, width, most, cuts=(), kind=jnp.bfloat16):
    drawn = jax.random.normal(key, dims, jnp.float32) * width
    if len(cuts) > 0:
        drawn = shard_levels(key, dims, cuts, -0.22, 0.18) * drawn
    return jnp.clip(drawn, min=-most, max=most).astype(kind)


def setup_inputs(seed: int = 0) -> dict:
    splits = jax.random.split(jax.random.key(seed), 6)
    return {
        "geometry": draw_geometry(jax.random.fold_in(splits[5], 71), 0),
        "panel": centred(splits[1], (FILAMENTS, COLS), 1.0, 6.0, ((0, 128),)),
        "pair_first": touch_ends(jax.random.randint(splits[2], (PAIRS,), 0, BLK_DEV), jax.random.fold_in(splits[2], 1), 0, BLK_DEV - 1).astype(jnp.int32),
        "pair_second": draw_pair_second(jax.random.fold_in(splits[5], 71), 0),
        "pair_count": draw_pair_count(jax.random.fold_in(splits[5], 71), 0),
    }


def make_tiles(geo_rows, geo_cols, valid_mask):
    diff_x = geo_rows[:, 0, :, None] - geo_cols[:, 0, None, :]
    diff_y = geo_rows[:, 1, :, None] - geo_cols[:, 1, None, :]
    diff_z = geo_rows[:, 2, :, None] - geo_cols[:, 2, None, :]
    reach_sum = geo_rows[:, 7, :, None] + geo_cols[:, 7, None, :]
    aligned = geo_rows[:, 3, :, None] * geo_cols[:, 3, None, :] + geo_rows[:, 4, :, None] * geo_cols[:, 4, None, :] + geo_rows[:, 5, :, None] * geo_cols[:, 5, None, :]
    weight = geo_rows[:, 6, :, None] * geo_cols[:, 6, None, :]
    spread = diff_x * diff_x + diff_y * diff_y + diff_z * diff_z + reach_sum * reach_sum
    values = BLOCK ** (-0.5) * weight * aligned / jnp.sqrt(spread)
    return (values * valid_mask[:, None, None].astype(jnp.float32)).astype(jnp.bfloat16)

def reference(geometry, panel, pair_first, pair_second, pair_count):
    margin = ((1, 1), (1, 1), (0, 0), (0, 0), (0, 0))
    geo_grid = geometry.reshape(8, GRID_X, GRID_Y, BLK_DEV, BLOCK).transpose(1, 2, 3, 0, 4)
    geo_grid = jnp.pad(geo_grid, margin)
    pan_grid = jnp.pad(panel.reshape(GRID_X, GRID_Y, BLK_DEV, BLOCK, COLS), margin)
    first_all = pair_first.reshape(GRID_X * GRID_Y, PAIR_DEV)
    second_all = pair_second.reshape(GRID_X * GRID_Y, PAIR_DEV)
    lane_ids = jnp.arange(GROUP, dtype=jnp.int32)
    centre_slot = 4 * BLK_DEV
    anchor = jnp.zeros((), jnp.int32)

    def device_step(totals, device):
        dev_x = (device // GRID_Y).astype(jnp.int32)
        dev_y = (device % GRID_Y).astype(jnp.int32)
        corner = (dev_x, dev_y, anchor, anchor, anchor)
        geo_near = lax.dynamic_slice(geo_grid, corner, (3, 3, BLK_DEV, 8, BLOCK)).reshape(9 * BLK_DEV, 8, BLOCK)
        pan_near = lax.dynamic_slice(pan_grid, corner, (3, 3, BLK_DEV, BLOCK, COLS)).reshape(9 * BLK_DEV, BLOCK, COLS)
        first_row = first_all[device]
        second_row = second_all[device]
        pair_total = pair_count[device]

        def group_step(carry_pair, group_index):
            own_rows, back_rows = carry_pair
            offset = (group_index * GROUP).astype(jnp.int32)
            first_ids = lax.dynamic_slice_in_dim(first_row, offset, GROUP)
            second_ids = lax.dynamic_slice_in_dim(second_row, offset, GROUP)
            row_ids = centre_slot + first_ids
            tiles = make_tiles(geo_near[row_ids], geo_near[second_ids], offset + lane_ids < pair_total).astype(jnp.float32)
            forward = jnp.einsum('gij,gjc->gic', tiles, pan_near[second_ids].astype(jnp.float32))
            keep_mask = (second_ids != row_ids).astype(jnp.float32)[:, None, None]
            backward = jnp.einsum('gij,gic->gjc', tiles, pan_near[row_ids].astype(jnp.float32)) * keep_mask
            return ((own_rows.at[first_ids].add(forward), back_rows.at[second_ids].add(backward)), None)
        start_pair = (jnp.zeros((BLK_DEV, BLOCK, COLS), jnp.float32), jnp.zeros((9 * BLK_DEV, BLOCK, COLS), jnp.float32))
        own_rows, back_rows = lax.scan(group_step, start_pair, jnp.arange(PAIR_DEV // GROUP, dtype=jnp.int32))[0]
        back_rows = back_rows.reshape(3, 3, BLK_DEV, BLOCK, COLS)
        shares = lax.optimization_barrier(back_rows.astype(jnp.bfloat16)).astype(jnp.float32)
        shares = shares.at[1, 1].set(own_rows + back_rows[1, 1])
        window = lax.dynamic_slice(totals, corner, (3, 3, BLK_DEV, BLOCK, COLS))
        return (lax.dynamic_update_slice(totals, window + shares, corner), None)
    totals = jnp.zeros((GRID_X + 2, GRID_Y + 2, BLK_DEV, BLOCK, COLS), jnp.float32)
    totals = lax.scan(device_step, totals, jnp.arange(GRID_X * GRID_Y, dtype=jnp.int32))[0]
    return totals[1:-1, 1:-1].reshape(GRID_X * GRID_Y * BLK_DEV * BLOCK, COLS)
```

```python
import functools

import jax
import jax.numpy as jnp
from jax import lax
from jax.experimental import pallas as pl
from jax.experimental.pallas import tpu as pltpu
from jax.sharding import PartitionSpec as P

BLOCK = 512
GEO_ROWS = 16
LANES = 128
CHUNK = 32
CODES = 64
F32 = jnp.float32
BF16 = jnp.bfloat16


def halves(values):
    high = values.astype(BF16).astype(F32)
    return high, (values - high).astype(BF16).astype(F32)


def pack_kernel(place, geometry, slots, panel, payload, geo_tiles, sems):
    fil_dev = geometry.shape[1]
    rows = panel.shape[0]
    panel_copy = pltpu.make_async_copy(panel, payload.at[pl.ds(0, rows), :], sems.at[0])
    panel_copy.start()
    moment = geometry[3:6, :] * geometry[6:7, :]
    moment_high, moment_low = halves(moment)
    x_high, x_low = halves(geometry[0:1, :] - place[0])
    y_high, y_low = halves(geometry[1:2, :] - place[1])
    z = geometry[2:3, :]
    z_high, z_mid = halves(z)
    z_low = ((z - z_high) - z_mid).astype(BF16).astype(F32)
    a_high, a_low = halves(geometry[7:8, :])
    info = jnp.concatenate(
        [slots[0:1, :], slots[1:2, :], jnp.zeros((1, fil_dev - 2 * LANES), F32)], axis=1
    )
    pieces = jnp.concatenate(
        [moment_high, moment_low, x_high, x_low, y_high, y_low, z_high, z_mid, z_low, a_high, a_low, info],
        axis=0,
    ).astype(BF16)
    for tile in range(fil_dev // LANES):
        geo_tiles[tile * GEO_ROWS : (tile + 1) * GEO_ROWS, :] = pieces[:, tile * LANES : (tile + 1) * LANES]
    geo_copy = pltpu.make_async_copy(geo_tiles, payload.at[pl.ds(rows, geo_tiles.shape[0]), :], sems.at[1])
    geo_copy.start()
    panel_copy.wait()
    geo_copy.wait()


def geo_block(message, start):
    tiles = BLOCK // LANES
    return jnp.concatenate(
        [message[pl.ds(pl.multiple_of(start + t * GEO_ROWS, GEO_ROWS), GEO_ROWS), :] for t in range(tiles)],
        axis=1,
    )


def positions(geo):
    return (
        geo[6:7] + geo[7:8],
        geo[8:9] + geo[9:10],
        geo[10:11] + geo[11:12] + geo[12:13],
        geo[13:14] + geo[14:15],
    )


def make_columns(message, panel_rows, columns, moments):
    per_block = BLOCK // LANES * GEO_ROWS
    for block in range(panel_rows // BLOCK):
        geo = geo_block(message, panel_rows + block * per_block).astype(F32)
        spots = jnp.concatenate(positions(geo) + (jnp.zeros((4, BLOCK), F32),), axis=0)
        columns[pl.ds(block * BLOCK, BLOCK), :] = spots.T
        high, low = halves((geo[0:3] + geo[3:6]) * BLOCK ** (-0.5))
        gap = jnp.zeros((10, BLOCK), F32)
        stacked = jnp.concatenate([high, high, gap, low, low, gap], axis=0)
        moments[pl.ds(block * BLOCK, BLOCK), :] = stacked.T.astype(BF16)


def phase_kernel(offsets, local, rows, *refs):
    count = len(offsets)
    panel_rows = rows[1]
    message_rows = rows[0]
    sources, refs = refs[: rows[2]], refs[rows[2] :]
    if local:
        columns_out, moments_out, total = refs[:3]
        columns, moments = columns_out, moments_out
        refs = refs[3:]
    else:
        own_info, columns, moments, total_in, total = refs[:5]
        refs = refs[5:]
    message, counts, counts_s, items, tile_even, tile_odd, sems, count_sem = refs
    per_source = count // rows[2]
    copies = []
    for index, source in enumerate(sources):
        size = per_source * message_rows
        copies.append(
            pltpu.make_async_copy(source, message.at[pl.ds(index * size, size), :], sems.at[index])
        )
        copies[-1].start()
    if local:
        total[...] = jnp.zeros_like(total)
    else:
        total[...] = total_in[...]
    tile_odd[...] = jnp.zeros_like(tile_odd)
    for copy in copies:
        copy.wait()
    if local:
        make_columns(message, panel_rows, columns, moments)

    def info_of(ref, start):
        return ref[start : start + 16, :].astype(F32)[15:16], ref[start + 16 : start + 32, :].astype(F32)[15:16]

    lane = lax.broadcasted_iota(jnp.int32, (1, LANES), 1)
    own_first, own_second = info_of(message, panel_rows) if local else info_of(own_info, 0)
    codes = []
    for index, (step_x, step_y) in enumerate(offsets):
        near = (step_x + 1) * 3 + step_y + 1
        far_first, far_second = (
            (own_first, own_second) if local else info_of(message, index * message_rows + panel_rows)
        )
        own_block = own_second - (1.0 + 8 * near)
        far_block = far_second - (1.0 + 8 * (8 - near))
        own_fits = (own_block >= 0.0) & (own_block < 8.0)
        far_fits = (far_block >= 0.0) & (far_block < 8.0)
        if local:
            far_fits = far_fits & (far_block != far_first)
        own_code = jnp.where(own_fits, own_first * 8.0 + own_block, -1.0)
        far_code = jnp.where(far_fits, far_block * 8.0 + far_first, -1.0)
        codes.append(jnp.where(lane < CODES, own_code, far_code))
    row = lax.broadcasted_iota(jnp.int32, (CODES, LANES), 0).astype(F32)
    hits = jnp.concatenate([(row == code).astype(F32) for code in codes], axis=0).astype(BF16)
    counts[...] = lax.dot_general(
        jnp.ones((8, LANES), BF16), hits, (((1,), (1,)), ((), ())), preferred_element_type=F32
    ).astype(jnp.int32)
    count_copy = pltpu.make_async_copy(counts, counts_s, count_sem)
    count_copy.start()
    count_copy.wait()

    def gather(code, used):
        often = counts_s[0, code]
        items[used] = code + often * 1024
        return used + jnp.minimum(often, 1)

    used = lax.fori_loop(0, count * CODES, gather, jnp.int32(0), unroll=8)
    items[used] = 0
    items[used + 1] = 0

    def decode(item):
        code = item & 1023
        return code >> 6, (code >> 3) & 7, code & 7, (item >> 10).astype(F32)

    def build(item, tile):
        source, mine, block, _ = decode(item)
        first_row = pl.multiple_of(mine * BLOCK, BLOCK)
        geo = geo_block(
            message, source * message_rows + panel_rows + block * (BLOCK // LANES * GEO_ROWS)
        )
        weights = jnp.concatenate([geo, geo], axis=0)
        near_x, near_y, near_z, near_a = positions(geo.astype(F32))
        step_x, step_y = F32(offsets[0][0]), F32(offsets[0][1])
        for index in range(1, count):
            step_x = jnp.where(source == index, F32(offsets[index][0]), step_x)
            step_y = jnp.where(source == index, F32(offsets[index][1]), step_y)
        near_x = near_x + step_x
        near_y = near_y + step_y
        spots = columns[pl.ds(first_row, BLOCK), :]
        moment = moments[pl.ds(first_row, BLOCK), :]
        for start in range(0, BLOCK, CHUNK):
            spot = spots[start : start + CHUNK]
            aligned = jnp.dot(moment[start : start + CHUNK], weights, preferred_element_type=F32)
            diff_x = spot[:, 0:1] - near_x
            diff_y = spot[:, 1:2] - near_y
            diff_z = spot[:, 2:3] - near_z
            reach = spot[:, 3:4] + near_a
            spread = diff_x * diff_x + diff_y * diff_y + diff_z * diff_z + reach * reach
            tile[start : start + CHUNK, :] = (aligned * lax.rsqrt(spread)).astype(BF16)

    def apply(item, tile, scale):
        source, mine, block, often = decode(item)
        near_panel = message[
            pl.ds(pl.multiple_of(source * message_rows + block * BLOCK, BLOCK), BLOCK), :
        ]
        product = jnp.dot(tile[...], near_panel, preferred_element_type=F32)
        span = pl.ds(pl.multiple_of(mine * BLOCK, BLOCK), BLOCK)
        total[span, :] += product * (often * scale)

    def step(index, last):
        even, odd = items[2 * index], items[2 * index + 1]
        apply(last, tile_odd, 1.0)
        build(even, tile_even)
        apply(even, tile_even, 1.0)
        build(odd, tile_odd)
        return odd

    last = lax.fori_loop(0, (used + 1) // 2, step, jnp.int32(0))
    apply(last, tile_odd, 1.0)


def phase(offsets, sources, message_rows, panel_rows, others):
    local = not others
    count = len(offsets)
    rows = (message_rows, panel_rows, len(sources))
    whole = pl.BlockSpec(memory_space=pltpu.VMEM)
    anywhere = pl.BlockSpec(memory_space=pl.ANY)
    total = jax.ShapeDtypeStruct((panel_rows, LANES), F32)
    if local:
        out_shape = (
            jax.ShapeDtypeStruct((panel_rows, 8), F32),
            jax.ShapeDtypeStruct((panel_rows, 32), BF16),
            total,
        )
        out_specs = (whole, whole, whole)
        aliases = {}
    else:
        out_shape, out_specs = total, whole
        aliases = {len(sources) + len(others) - 1: 0}
    return pl.pallas_call(
        functools.partial(phase_kernel, offsets, local, rows),
        out_shape=out_shape,
        in_specs=[anywhere] * len(sources) + [whole] * len(others),
        out_specs=out_specs,
        scratch_shapes=[
            pltpu.VMEM((count * message_rows, LANES), BF16),
            pltpu.VMEM((8, count * CODES), jnp.int32),
            pltpu.SMEM((8, count * CODES), jnp.int32),
            pltpu.SMEM((count * CODES + 2,), jnp.int32),
            pltpu.VMEM((BLOCK, BLOCK), BF16),
            pltpu.VMEM((BLOCK, BLOCK), BF16),
            pltpu.SemaphoreType.DMA((len(sources),)),
            pltpu.SemaphoreType.DMA,
        ],
        input_output_aliases=aliases,
        compiler_params=pltpu.CompilerParams(vmem_limit_bytes=40 * 2**20),
        name="near_" + str(count) + ("_own" if local else ""),
    )(*sources, *others)


def shifted(array, axis, by):
    devices = lax.axis_size(axis)
    pairs = [(i, i + by) for i in range(devices) if 0 <= i + by < devices]
    return lax.ppermute(array, axis, pairs)


def shards(geometry, panel, pair_first, pair_second, pair_count):
    panel_rows = panel.shape[0]
    message_rows = panel_rows + geometry.shape[1] // LANES * GEO_ROWS
    place = jnp.stack([lax.axis_index("gx"), lax.axis_index("gy")]).astype(F32) + 0.5
    used = jnp.arange(pair_first.shape[0], dtype=jnp.int32) < pair_count[0]
    second = jnp.where(used, pair_second + 1, 0)
    slots = jnp.stack([jnp.tile(pair_first, 2), jnp.tile(second, 2)]).astype(F32)
    whole = pl.BlockSpec(memory_space=pltpu.VMEM)
    anywhere = pl.BlockSpec(memory_space=pl.ANY)
    message = pl.pallas_call(
        pack_kernel,
        out_shape=jax.ShapeDtypeStruct((message_rows, LANES), BF16),
        in_specs=[pl.BlockSpec(memory_space=pltpu.SMEM), whole, whole, anywhere],
        out_specs=anywhere,
        scratch_shapes=[
            pltpu.VMEM((message_rows - panel_rows, LANES), BF16),
            pltpu.SemaphoreType.DMA((2,)),
        ],
        name="pack",
    )(place, geometry, slots, panel)
    from_left, from_right = shifted(message, "gx", 1), shifted(message, "gx", -1)
    from_below, from_above = shifted(message, "gy", 1), shifted(message, "gy", -1)
    columns, moments, total = phase(((0, 0),), (message,), message_rows, panel_rows, ())
    info = lax.slice_in_dim(message, panel_rows, panel_rows + 32, axis=0)
    both = jnp.concatenate([from_left, from_right], axis=0)
    corners_below, corners_above = shifted(both, "gy", 1), shifted(both, "gy", -1)
    total = phase(
        ((0, -1), (0, 1)), (from_below, from_above), message_rows, panel_rows,
        (info, columns, moments, total),
    )
    total = phase(
        ((-1, 0), (1, 0)), (from_left, from_right), message_rows, panel_rows,
        (info, columns, moments, total),
    )
    return phase(
        ((-1, -1), (1, -1), (-1, 1), (1, 1)), (corners_below, corners_above), message_rows, panel_rows,
        (info, columns, moments, total),
    )


def solution(mesh):
    in_specs = (
        P(None, ("gx", "gy")),
        P(("gx", "gy"), None),
        P(("gx", "gy")),
        P(("gx", "gy")),
        P(("gx", "gy")),
    )
    out_specs = P(("gx", "gy"), None)
    return jax.shard_map(shards, mesh=mesh, in_specs=in_specs, out_specs=out_specs, check_vma=False)
```

```python
import functools

import jax
import jax.numpy as jnp
from jax import lax
from jax.experimental import pallas as pl
from jax.experimental.pallas import tpu as pltpu
from jax.sharding import PartitionSpec as P

BLOCK = 512
GEO_ROWS = 16
LANES = 128
CHUNK = 32
CODES = 64
F32 = jnp.float32
BF16 = jnp.bfloat16


def halves(values):
    high = values.astype(BF16).astype(F32)
    return high, (values - high).astype(BF16).astype(F32)


def pack_kernel(first, second, used, geometry, panel, message, sem):
    fil_dev = geometry.shape[1]
    rows = panel.shape[0]
    panel_copy = pltpu.make_async_copy(panel, message.at[pl.ds(0, rows), :], sem)
    panel_copy.start()
    moment_high, moment_low = halves(geometry[3:6, :] * geometry[6:7, :])
    x_high, x_low = halves(geometry[0:1, :] - (lax.axis_index("gx").astype(F32) + 0.5))
    y_high, y_low = halves(geometry[1:2, :] - (lax.axis_index("gy").astype(F32) + 0.5))
    z = geometry[2:3, :]
    z_high, z_mid = halves(z)
    z_low = ((z - z_high) - z_mid).astype(BF16).astype(F32)
    a_high, a_low = halves(geometry[7:8, :])
    slot = lax.broadcasted_iota(jnp.int32, second.shape, 1)
    near = jnp.where(slot < used[0], second[...] + 1, 0).astype(F32)
    mine = first[...].astype(F32)
    info = jnp.concatenate([mine, mine, near, near, jnp.zeros((1, fil_dev - 2 * LANES), F32)], axis=1)
    pieces = jnp.concatenate(
        [moment_high, moment_low, x_high, x_low, y_high, y_low, z_high, z_mid, z_low, a_high, a_low, info],
        axis=0,
    ).astype(BF16)
    for tile in range(fil_dev // LANES):
        start = rows + tile * GEO_ROWS
        message[start : start + GEO_ROWS, :] = pieces[:, tile * LANES : (tile + 1) * LANES]
    panel_copy.wait()


def geo_block(message, start):
    tiles = BLOCK // LANES
    return jnp.concatenate(
        [message[pl.ds(pl.multiple_of(start + t * GEO_ROWS, GEO_ROWS), GEO_ROWS), :] for t in range(tiles)],
        axis=1,
    )


def positions(geo):
    return (
        geo[6:7] + geo[7:8],
        geo[8:9] + geo[9:10],
        geo[10:11] + geo[11:12] + geo[12:13],
        geo[13:14] + geo[14:15],
    )


def make_columns(message, panel_rows, columns, moments):
    per_block = BLOCK // LANES * GEO_ROWS
    for block in range(panel_rows // BLOCK):
        geo = geo_block(message, panel_rows + block * per_block).astype(F32)
        spots = jnp.concatenate(positions(geo) + (jnp.zeros((4, BLOCK), F32),), axis=0)
        columns[pl.ds(block * BLOCK, BLOCK), :] = spots.T
        high, low = halves((geo[0:3] + geo[3:6]) * BLOCK ** (-0.5))
        gap = jnp.zeros((10, BLOCK), F32)
        stacked = jnp.concatenate([high, high, gap, low, low, gap], axis=0)
        moments[pl.ds(block * BLOCK, BLOCK), :] = stacked.T.astype(BF16)


def phase_kernel(offsets, local, rows, *refs):
    count = len(offsets)
    panel_rows = rows[1]
    message_rows = rows[0]
    sources, refs = refs[: rows[2]], refs[rows[2] :]
    if local:
        columns_out, moments_out, total = refs[:3]
        columns, moments = columns_out, moments_out
        refs = refs[3:]
    else:
        own_info, columns, moments, total_in, total = refs[:5]
        refs = refs[5:]
    message, infos, counts, counts_s, items, tile_even, tile_odd, sems, info_sems, count_sem = refs
    per_source = count // rows[2]
    copies, info_copies = [], []
    for index in range(0 if local else count):
        start = index % per_source * message_rows + panel_rows
        info_copies.append(
            pltpu.make_async_copy(
                sources[index // per_source].at[pl.ds(start, 32), :],
                infos.at[pl.ds(index * 32, 32), :],
                info_sems.at[index],
            )
        )
        info_copies[-1].start()
    for index, source in enumerate(sources):
        size = per_source * message_rows
        copies.append(
            pltpu.make_async_copy(source, message.at[pl.ds(index * size, size), :], sems.at[index])
        )
        copies[-1].start()
    if local:
        total[...] = jnp.zeros_like(total)
    else:
        total[...] = total_in[...]
    tile_odd[...] = jnp.zeros_like(tile_odd)
    if local:
        copies.pop().wait()
        make_columns(message, panel_rows, columns, moments)

    for copy in info_copies:
        copy.wait()

    def info_of(ref, start):
        return ref[start : start + 16, :].astype(F32)[15:16], ref[start + 16 : start + 32, :].astype(F32)[15:16]

    lane = lax.broadcasted_iota(jnp.int32, (1, LANES), 1)
    own_first, own_second = info_of(message, panel_rows) if local else info_of(own_info, 0)
    codes = []
    for index, (step_x, step_y) in enumerate(offsets):
        near = (step_x + 1) * 3 + step_y + 1
        far_first, far_second = (
            (own_first, own_second) if local else info_of(infos, index * 32)
        )
        own_block = own_second - (1.0 + 8 * near)
        far_block = far_second - (1.0 + 8 * (8 - near))
        own_fits = (own_block >= 0.0) & (own_block < 8.0)
        far_fits = (far_block >= 0.0) & (far_block < 8.0)
        if local:
            far_fits = far_fits & (far_block != far_first)
        own_code = jnp.where(own_fits, own_first * 8.0 + own_block, -1.0)
        far_code = jnp.where(far_fits, far_block * 8.0 + far_first, -1.0)
        codes.append(jnp.where(lane < CODES, own_code, far_code))
    row = lax.broadcasted_iota(jnp.int32, (CODES, LANES), 0).astype(F32)
    hits = jnp.concatenate([(row == code).astype(F32) for code in codes], axis=0).astype(BF16)
    counts[...] = lax.dot_general(
        jnp.ones((8, LANES), BF16), hits, (((1,), (1,)), ((), ())), preferred_element_type=F32
    ).astype(jnp.int32)
    count_copy = pltpu.make_async_copy(counts, counts_s, count_sem)
    count_copy.start()
    count_copy.wait()

    def gather(code, used):
        often = counts_s[0, code]
        items[used] = code + often * 1024
        return used + jnp.minimum(often, 1)

    used = lax.fori_loop(0, count * CODES, gather, jnp.int32(0), unroll=8)
    items[used] = 0
    items[used + 1] = 0

    for copy in copies:
        copy.wait()

    def decode(item):
        code = item & 1023
        return code >> 6, (code >> 3) & 7, code & 7, (item >> 10).astype(F32)

    def build(item, tile):
        source, mine, block, _ = decode(item)
        first_row = pl.multiple_of(mine * BLOCK, BLOCK)
        geo = geo_block(
            message, source * message_rows + panel_rows + block * (BLOCK // LANES * GEO_ROWS)
        )
        weights = jnp.concatenate([geo, geo], axis=0)
        near_x, near_y, near_z, near_a = positions(geo.astype(F32))
        step_x, step_y = F32(offsets[0][0]), F32(offsets[0][1])
        for index in range(1, count):
            step_x = jnp.where(source == index, F32(offsets[index][0]), step_x)
            step_y = jnp.where(source == index, F32(offsets[index][1]), step_y)
        near_x = near_x + step_x
        near_y = near_y + step_y
        spots = columns[pl.ds(first_row, BLOCK), :]
        moment = moments[pl.ds(first_row, BLOCK), :]
        for start in range(0, BLOCK, CHUNK):
            spot = spots[start : start + CHUNK]
            aligned = jnp.dot(moment[start : start + CHUNK], weights, preferred_element_type=F32)
            diff_x = spot[:, 0:1] - near_x
            diff_y = spot[:, 1:2] - near_y
            diff_z = spot[:, 2:3] - near_z
            reach = spot[:, 3:4] + near_a
            spread = diff_x * diff_x + diff_y * diff_y + diff_z * diff_z + reach * reach
            tile[start : start + CHUNK, :] = (aligned * lax.rsqrt(spread)).astype(BF16)

    def apply(item, tile, scale):
        source, mine, block, often = decode(item)
        near_panel = message[
            pl.ds(pl.multiple_of(source * message_rows + block * BLOCK, BLOCK), BLOCK), :
        ]
        product = jnp.dot(tile[...], near_panel, preferred_element_type=F32)
        span = pl.ds(pl.multiple_of(mine * BLOCK, BLOCK), BLOCK)
        total[span, :] += product * (often * scale)

    def step(index, last):
        even, odd = items[2 * index], items[2 * index + 1]
        apply(last, tile_odd, 1.0)
        build(even, tile_even)
        apply(even, tile_even, 1.0)
        build(odd, tile_odd)
        return odd

    last = lax.fori_loop(0, (used + 1) // 2, step, jnp.int32(0))
    apply(last, tile_odd, 1.0)


def phase(offsets, sources, message_rows, panel_rows, others):
    local = not others
    count = len(offsets)
    rows = (message_rows, panel_rows, len(sources))
    whole = pl.BlockSpec(memory_space=pltpu.VMEM)
    anywhere = pl.BlockSpec(memory_space=pl.ANY)
    total = jax.ShapeDtypeStruct((panel_rows, LANES), F32)
    if local:
        out_shape = (
            jax.ShapeDtypeStruct((panel_rows, 8), F32),
            jax.ShapeDtypeStruct((panel_rows, 32), BF16),
            total,
        )
        out_specs = (whole, whole, whole)
        aliases = {}
    else:
        out_shape, out_specs = total, whole
        aliases = {len(sources) + len(others) - 1: 0}
    return pl.pallas_call(
        functools.partial(phase_kernel, offsets, local, rows),
        out_shape=out_shape,
        in_specs=[anywhere] * len(sources) + [whole] * len(others),
        out_specs=out_specs,
        scratch_shapes=[
            pltpu.VMEM((count * message_rows, LANES), BF16),
            pltpu.VMEM((count * 32, LANES), BF16),
            pltpu.VMEM((8, count * CODES), jnp.int32),
            pltpu.SMEM((8, count * CODES), jnp.int32),
            pltpu.SMEM((count * CODES + 2,), jnp.int32),
            pltpu.VMEM((BLOCK, BLOCK), BF16),
            pltpu.VMEM((BLOCK, BLOCK), BF16),
            pltpu.SemaphoreType.DMA((len(sources),)),
            pltpu.SemaphoreType.DMA((count,)),
            pltpu.SemaphoreType.DMA,
        ],
        input_output_aliases=aliases,
        compiler_params=pltpu.CompilerParams(vmem_limit_bytes=(14 + 2 * count) * 2**20),
        name="near_" + str(count) + ("_own" if local else ""),
    )(*sources, *others)


def shifted(array, axis, by):
    devices = lax.axis_size(axis)
    pairs = [(i, i + by) for i in range(devices) if 0 <= i + by < devices]
    return lax.ppermute(array, axis, pairs)


def shards(geometry, panel, pair_first, pair_second, pair_count):
    panel_rows = panel.shape[0]
    message_rows = panel_rows + geometry.shape[1] // LANES * GEO_ROWS
    slots = pair_first.shape[0]
    whole = pl.BlockSpec(memory_space=pltpu.VMEM)
    message = pl.pallas_call(
        pack_kernel,
        out_shape=jax.ShapeDtypeStruct((message_rows, LANES), BF16),
        in_specs=[whole, whole, pl.BlockSpec(memory_space=pltpu.SMEM), whole, pl.BlockSpec(memory_space=pl.ANY)],
        out_specs=whole,
        scratch_shapes=[pltpu.SemaphoreType.DMA],
        compiler_params=pltpu.CompilerParams(vmem_limit_bytes=8 * 2**20),
        name="pack",
    )(pair_first.reshape(1, slots), pair_second.reshape(1, slots), pair_count, geometry, panel)
    from_left, from_right = shifted(message, "gx", 1), shifted(message, "gx", -1)
    from_below, from_above = shifted(message, "gy", 1), shifted(message, "gy", -1)
    columns, moments, total = phase(((0, 0),), (message,), message_rows, panel_rows, ())
    info = lax.slice_in_dim(message, panel_rows, panel_rows + 32, axis=0)
    total = phase(
        ((0, -1), (0, 1)), (from_below, from_above), message_rows, panel_rows,
        (info, columns, moments, total),
    )
    from_left, from_right, total = lax.optimization_barrier((from_left, from_right, total))
    both = jnp.concatenate([from_left, from_right], axis=0)
    corners_below, corners_above = shifted(both, "gy", 1), shifted(both, "gy", -1)
    total = phase(
        ((-1, 0), (1, 0)), (from_left, from_right), message_rows, panel_rows,
        (info, columns, moments, total),
    )
    return phase(
        ((-1, -1), (1, -1), (-1, 1), (1, 1)), (corners_below, corners_above), message_rows, panel_rows,
        (info, columns, moments, total),
    )


def solution(mesh):
    in_specs = (
        P(None, ("gx", "gy")),
        P(("gx", "gy"), None),
        P(("gx", "gy")),
        P(("gx", "gy")),
        P(("gx", "gy")),
    )
    out_specs = P(("gx", "gy"), None)
    return jax.shard_map(shards, mesh=mesh, in_specs=in_specs, out_specs=out_specs, check_vma=False)
```

```python
import functools

import jax
import jax.numpy as jnp
from jax import lax
from jax.experimental import pallas as pl
from jax.experimental.pallas import tpu as pltpu
from jax.sharding import PartitionSpec as P

BLOCK = 512
GEO_ROWS = 16
LANES = 128
CHUNK = 64
EARLY = 14
CODES = 64
F32 = jnp.float32
BF16 = jnp.bfloat16


def halves(values):
    high = values.astype(BF16).astype(F32)
    return high, (values - high).astype(BF16).astype(F32)


def thirds(values):
    high = values.astype(BF16).astype(F32)
    rest = values - high
    middle = rest.astype(BF16).astype(F32)
    return jnp.concatenate([high, middle, (rest - middle).astype(BF16).astype(F32)], axis=0)


def pack_kernel(used, first_in, second_in, geometry_in, panel, message, first, second, geometry, sems):
    fil_dev = geometry.shape[1]
    rows = panel.shape[0]
    pairs = ((panel, message.at[pl.ds(0, rows), :]), (first_in, first), (second_in, second), (geometry_in, geometry))
    copies = [pltpu.make_async_copy(source, target, sems.at[n]) for n, (source, target) in enumerate(pairs)]
    for copy in copies:
        copy.start()
    for copy in copies[1:]:
        copy.wait()
    moment_high, moment_low = halves(geometry[3:6, :] * geometry[6:7, :])
    x_high, x_low = halves(geometry[0:1, :] - (lax.axis_index("gx").astype(F32) + 0.5))
    y_high, y_low = halves(geometry[1:2, :] - (lax.axis_index("gy").astype(F32) + 0.5))
    z = geometry[2:3, :]
    z_high, z_mid = halves(z)
    z_low = ((z - z_high) - z_mid).astype(BF16).astype(F32)
    a_high, a_low = halves(geometry[7:8, :])
    slot = lax.broadcasted_iota(jnp.int32, second.shape, 1)
    near = jnp.where(slot < used[0], second[...] + 1, 0).astype(F32)
    mine = first[...].astype(F32)
    info = jnp.concatenate([mine, mine, near, near, jnp.zeros((1, fil_dev - 2 * LANES), F32)], axis=1)
    pieces = jnp.concatenate(
        [moment_high, moment_low, x_high, x_low, y_high, y_low, z_high, z_mid, z_low, a_high, a_low, info],
        axis=0,
    ).astype(BF16)
    for tile in range(fil_dev // LANES):
        start = rows + tile * GEO_ROWS
        message[start : start + GEO_ROWS, :] = pieces[:, tile * LANES : (tile + 1) * LANES]
    copies[0].wait()


def geo_block(message, start):
    tiles = BLOCK // LANES
    return jnp.concatenate(
        [message[pl.ds(pl.multiple_of(start + t * GEO_ROWS, GEO_ROWS), GEO_ROWS), :] for t in range(tiles)],
        axis=1,
    )


def positions(geo):
    return (
        geo[6:7] + geo[7:8],
        geo[8:9] + geo[9:10],
        geo[10:11] + geo[11:12] + geo[12:13],
        geo[13:14] + geo[14:15],
    )


def make_columns(message, panel_rows, columns, features):
    per_block = BLOCK // LANES * GEO_ROWS
    for block in range(panel_rows // BLOCK):
        geo = geo_block(message, panel_rows + block * per_block).astype(F32)
        here_x, here_y, here_z, here_a = positions(geo)
        spots = jnp.concatenate([here_x, here_y, here_z, here_a, jnp.zeros((4, BLOCK), F32)], axis=0)
        columns[pl.ds(block * BLOCK, BLOCK), :] = spots.T
        high, low = halves((geo[0:3] + geo[3:6]) * BLOCK ** (-0.5))
        gap = jnp.zeros((10, BLOCK), F32)
        parts = [high, high, gap, low, low, gap]
        for piece in (0, 1):
            at_x, at_y, at_a = (geo[k + piece : k + piece + 1] for k in (6, 8, 13))
            hole = jnp.zeros((6, BLOCK), F32)
            parts += [hole, -2.0 * at_x, -2.0 * at_x, -2.0 * at_y, -2.0 * at_y, hole[0:3]]
            parts += [2.0 * at_a, 2.0 * at_a, hole[0:1]]
        parts += [jnp.ones((3, BLOCK), F32), thirds(here_x * here_x + here_y * here_y + here_a * here_a)]
        parts += [-2.0 * geo[6:10], jnp.zeros((6, BLOCK), F32)]
        features[pl.ds(block * BLOCK, BLOCK), :] = jnp.concatenate(parts, axis=0).T.astype(BF16)


def stage_kernel(offsets, sizes, early, role, *refs):
    message_rows, panel_rows, per_source = sizes
    count = len(offsets)
    source_count = count // per_source
    sources, refs = refs[:source_count], refs[source_count:]
    if role == "first":
        columns, features, total = refs[:3]
        refs = refs[3:]
    else:
        own_info, columns, features, total_in, total = refs[:5]
        refs = refs[5:]
    message, infos, counts, counts_s, items, tile_even, tile_odd, sems, info_sems, count_sem = refs

    info_copies, copies = [], []
    for index in range(count):
        start = index % per_source * message_rows + panel_rows
        source = sources[index // per_source]
        info_copies.append(
            pltpu.make_async_copy(
                source.at[pl.ds(start, 32), :], infos.at[pl.ds(index * 32, 32), :], info_sems.at[index]
            )
        )
        info_copies[-1].start()
    for index in range(count):
        span = pl.ds(index % per_source * message_rows, message_rows)
        copies.append(
            pltpu.make_async_copy(
                sources[index // per_source].at[span, :],
                message.at[pl.ds(index * message_rows, message_rows), :],
                sems.at[index],
            )
        )
        copies[-1].start()
    if role == "first":
        total[...] = jnp.zeros_like(total)
    else:
        total[...] = total_in[...]
    tile_odd[...] = jnp.zeros_like(tile_odd)
    for copy in info_copies:
        copy.wait()

    def info_of(ref, start):
        return ref[start : start + 16, :].astype(F32)[15:16], ref[start + 16 : start + 32, :].astype(F32)[15:16]

    lane = lax.broadcasted_iota(jnp.int32, (1, LANES), 1)
    own_first, own_second = info_of(infos if role == "first" else own_info, 0)
    codes = []
    for index, (step_x, step_y) in enumerate(offsets):
        near = (step_x + 1) * 3 + step_y + 1
        far_first, far_second = info_of(infos, index * 32)
        own_block = own_second - (1.0 + 8 * near)
        far_block = far_second - (1.0 + 8 * (8 - near))
        own_fits = (own_block >= 0.0) & (own_block < 8.0)
        far_fits = (far_block >= 0.0) & (far_block < 8.0)
        if near == 4:
            far_fits = far_fits & (far_block != far_first)
        own_code = jnp.where(own_fits, own_first * 8.0 + own_block, -1.0)
        far_code = jnp.where(far_fits, far_block * 8.0 + far_first, -1.0)
        codes.append(jnp.where(lane < CODES, own_code, far_code))
    row = lax.broadcasted_iota(jnp.int32, (CODES, LANES), 0).astype(F32)
    hits = jnp.concatenate([(row == code).astype(F32) for code in codes], axis=0).astype(BF16)
    counts[...] = lax.dot_general(
        jnp.ones((8, LANES), BF16), hits, (((1,), (1,)), ((), ())), preferred_element_type=F32
    ).astype(jnp.int32)
    count_copy = pltpu.make_async_copy(counts, counts_s, count_sem)
    count_copy.start()
    if role == "first":
        copies[0].wait()
        make_columns(message, panel_rows, columns, features)
    count_copy.wait()

    def gather(code, used):
        often = counts_s[0, code]
        items[used] = code + often * 1024
        return used + jnp.minimum(often, 1)

    begin = jnp.int32(0)
    used = lax.fori_loop(0, early * CODES, gather, jnp.int32(0), unroll=8)
    if role == "first":
        used = jnp.minimum(used, EARLY)
    else:
        begin = jnp.minimum(used, EARLY)
        used = lax.fori_loop(early * CODES, count * CODES, gather, used, unroll=8)
    items[used] = 0
    items[used + 1] = 0

    def decode(item):
        code = item & 1023
        return code >> 6, (code >> 3) & 7, code & 7, (item >> 10).astype(F32)

    def build(item, tile):
        source, mine, block, _ = decode(item)
        first_row = pl.multiple_of(mine * BLOCK, BLOCK)
        geo = geo_block(
            message, source * message_rows + panel_rows + block * (BLOCK // LANES * GEO_ROWS)
        )
        near_x, near_y, near_z, near_a = positions(geo.astype(F32))
        step_x, step_y = F32(offsets[0][0]), F32(offsets[0][1])
        for index in range(1, count):
            step_x = jnp.where(source == index, F32(offsets[index][0]), step_x)
            step_y = jnp.where(source == index, F32(offsets[index][1]), step_y)
        near_x = near_x + step_x
        near_y = near_y + step_y
        extra = jnp.concatenate(
            [
                thirds(near_x * near_x + near_y * near_y + near_a * near_a),
                jnp.ones((3, BLOCK), F32),
                jnp.full((2, BLOCK), step_x),
                jnp.full((2, BLOCK), step_y),
                jnp.zeros((6, BLOCK), F32),
            ],
            axis=0,
        ).astype(BF16)
        for_aligned = jnp.concatenate([geo, geo, jnp.zeros((48, BLOCK), BF16)], axis=0)
        for_spread = jnp.concatenate([jnp.zeros((32, BLOCK), BF16), geo, geo, extra], axis=0)
        spots = columns[pl.ds(first_row, BLOCK), :]
        feature = features[pl.ds(first_row, BLOCK), :]
        for turn, start in enumerate(range(0, BLOCK, CHUNK)):
            spot = spots[start : start + CHUNK]
            aligned = jnp.dot(feature[start : start + CHUNK], for_aligned, preferred_element_type=F32)
            diff_z = spot[:, 2:3] - near_z
            if turn % 2 == 1:
                spread = jnp.dot(feature[start : start + CHUNK], for_spread, preferred_element_type=F32)
                spread = spread + diff_z * diff_z
            else:
                diff_x = spot[:, 0:1] - near_x
                diff_y = spot[:, 1:2] - near_y
                reach = spot[:, 3:4] + near_a
                spread = diff_x * diff_x + diff_y * diff_y + diff_z * diff_z + reach * reach
            tile[start : start + CHUNK, :] = (aligned * lax.rsqrt(spread)).astype(BF16)

    def apply(item, tile):
        source, mine, block, often = decode(item)
        near_panel = message[
            pl.ds(pl.multiple_of(source * message_rows + block * BLOCK, BLOCK), BLOCK), :
        ]
        product = jnp.dot(tile[...], near_panel, preferred_element_type=F32)
        span = pl.ds(pl.multiple_of(mine * BLOCK, BLOCK), BLOCK)
        total[span, :] += product * often

    waited = 1 if role == "first" else 0

    def arrive(seen, needed):
        for index in range(waited, count):
            @pl.when((seen < index) & (index <= needed))
            def _(index=index):
                copies[index].wait()

    def step(index, carry):
        last, seen = carry
        even, odd = items[begin + 2 * index], items[begin + 2 * index + 1]
        needed = jnp.maximum(jnp.maximum(decode(even)[0], decode(odd)[0]), seen)
        arrive(seen, needed)
        apply(last, tile_odd)
        build(even, tile_even)
        apply(even, tile_even)
        build(odd, tile_odd)
        return odd, needed

    last, seen = lax.fori_loop(0, (used - begin + 1) // 2, step, (jnp.int32(0), jnp.int32(waited - 1)))
    arrive(seen, jnp.int32(count - 1))
    apply(last, tile_odd)


def stage(role, offsets, early, sources, sizes, others):
    count = len(offsets)
    message_rows, panel_rows, _ = sizes
    whole = pl.BlockSpec(memory_space=pltpu.VMEM)
    anywhere = pl.BlockSpec(memory_space=pl.ANY)
    out_shape, out_specs = jax.ShapeDtypeStruct((panel_rows, LANES), F32), whole
    if role == "first":
        out_shape = (
            jax.ShapeDtypeStruct((panel_rows, 8), F32),
            jax.ShapeDtypeStruct((panel_rows, 80), BF16),
            out_shape,
        )
        out_specs = (whole,) * 3
    return pl.pallas_call(
        functools.partial(stage_kernel, offsets, sizes, early, role),
        out_shape=out_shape,
        in_specs=[anywhere] * len(sources) + [whole] * len(others),
        out_specs=out_specs,
        scratch_shapes=[
            pltpu.VMEM((count * message_rows, LANES), BF16),
            pltpu.VMEM((count * 32, LANES), BF16),
            pltpu.VMEM((8, count * CODES), jnp.int32),
            pltpu.SMEM((8, count * CODES), jnp.int32),
            pltpu.SMEM((count * CODES + 2,), jnp.int32),
            pltpu.VMEM((BLOCK, BLOCK), BF16),
            pltpu.VMEM((BLOCK, BLOCK), BF16),
            pltpu.SemaphoreType.DMA((count,)),
            pltpu.SemaphoreType.DMA((count,)),
            pltpu.SemaphoreType.DMA,
        ],
        input_output_aliases={len(sources) + len(others) - 1: 0} if role == "second" else {},
        compiler_params=pltpu.CompilerParams(vmem_limit_bytes=(16 + 2 * count) * 2**20),
        name=role + "_stage",
    )(*sources, *others)


def shifted(array, axis, by):
    devices = lax.axis_size(axis)
    pairs = [(i, i + by) for i in range(devices) if 0 <= i + by < devices]
    return lax.ppermute(array, axis, pairs)


def shards(geometry, panel, pair_first, pair_second, pair_count):
    panel_rows = panel.shape[0]
    message_rows = panel_rows + geometry.shape[1] // LANES * GEO_ROWS
    slots = pair_first.shape[0]
    hbm = pl.BlockSpec(memory_space=pltpu.HBM)
    message = pl.pallas_call(
        pack_kernel,
        out_shape=jax.ShapeDtypeStruct((message_rows, LANES), BF16),
        in_specs=[pl.BlockSpec(memory_space=pltpu.SMEM), hbm, hbm, hbm, hbm],
        out_specs=pl.BlockSpec(memory_space=pltpu.VMEM),
        scratch_shapes=[
            pltpu.VMEM((1, slots), jnp.int32),
            pltpu.VMEM((1, slots), jnp.int32),
            pltpu.VMEM(geometry.shape, F32),
            pltpu.SemaphoreType.DMA((4,)),
        ],
        compiler_params=pltpu.CompilerParams(vmem_limit_bytes=8 * 2**20),
        name="pack",
    )(pair_count, pair_first.reshape(1, slots), pair_second.reshape(1, slots), geometry, panel)
    from_below, from_above = shifted(message, "gy", 1), shifted(message, "gy", -1)
    from_left, from_right = shifted(message, "gx", 1), shifted(message, "gx", -1)
    sizes = (message_rows, panel_rows, 1)
    beside = ((0, 0), (0, -1), (0, 1))
    nearest = (message, from_below, from_above)
    columns, features, total = stage("first", beside, 3, nearest, sizes, ())
    info = lax.slice_in_dim(message, panel_rows, panel_rows + 32, axis=0)
    from_left, from_right, total = lax.optimization_barrier((from_left, from_right, total))
    both = jnp.concatenate([from_left, from_right], axis=0)
    corners_below, corners_above = shifted(both, "gy", 1), shifted(both, "gy", -1)
    total = stage(
        "second", beside + ((-1, 0), (1, 0)), 3, nearest + (from_left, from_right), sizes,
        (info, columns, features, total),
    )
    return stage(
        "third", ((-1, -1), (1, -1), (-1, 1), (1, 1)), 0, (corners_below, corners_above),
        (message_rows, panel_rows, 2), (info, columns, features, total),
    )


def solution(mesh):
    in_specs = (
        P(None, ("gx", "gy")),
        P(("gx", "gy"), None),
        P(("gx", "gy")),
        P(("gx", "gy")),
        P(("gx", "gy")),
    )
    out_specs = P(("gx", "gy"), None)
    return jax.shard_map(shards, mesh=mesh, in_specs=in_specs, out_specs=out_specs, check_vma=False)
```

```python
import functools

import jax
import jax.numpy as jnp
from jax import lax
from jax.experimental import pallas as pl
from jax.experimental.pallas import tpu as pltpu
from jax.sharding import PartitionSpec as P

BLOCK = 512
GEO_ROWS = 16
LANES = 128
CHUNK = 64
EARLY = 22
ALONE = ("corner", "last")
CODES = 64
F32 = jnp.float32
BF16 = jnp.bfloat16


def halves(values):
    high = values.astype(BF16).astype(F32)
    return high, (values - high).astype(BF16).astype(F32)


def thirds(values):
    high = values.astype(BF16).astype(F32)
    rest = values - high
    middle = rest.astype(BF16).astype(F32)
    return jnp.concatenate([high, middle, (rest - middle).astype(BF16).astype(F32)], axis=0)


def pack_kernel(used, first_in, second_in, geometry_in, panel, message, first, second, geometry, sems):
    fil_dev = geometry.shape[1]
    rows = panel.shape[0]
    pairs = ((panel, message.at[pl.ds(0, rows), :]), (first_in, first), (second_in, second), (geometry_in, geometry))
    copies = [pltpu.make_async_copy(source, target, sems.at[n]) for n, (source, target) in enumerate(pairs)]
    for copy in copies:
        copy.start()
    for copy in copies[1:]:
        copy.wait()
    moment_high, moment_low = halves(geometry[3:6, :] * geometry[6:7, :])
    x_high, x_low = halves(geometry[0:1, :] - (lax.axis_index("gx").astype(F32) + 0.5))
    y_high, y_low = halves(geometry[1:2, :] - (lax.axis_index("gy").astype(F32) + 0.5))
    z = geometry[2:3, :]
    z_high, z_mid = halves(z)
    z_low = ((z - z_high) - z_mid).astype(BF16).astype(F32)
    a_high, a_low = halves(geometry[7:8, :])
    slot = lax.broadcasted_iota(jnp.int32, second.shape, 1)
    near = jnp.where(slot < used[0], second[...] + 1, 0).astype(F32)
    mine = first[...].astype(F32)
    info = jnp.concatenate([mine, mine, near, near, jnp.zeros((1, fil_dev - 2 * LANES), F32)], axis=1)
    pieces = jnp.concatenate(
        [moment_high, moment_low, x_high, x_low, y_high, y_low, z_high, z_mid, z_low, a_high, a_low, info],
        axis=0,
    ).astype(BF16)
    for tile in range(fil_dev // LANES):
        start = rows + tile * GEO_ROWS
        message[start : start + GEO_ROWS, :] = pieces[:, tile * LANES : (tile + 1) * LANES]
    copies[0].wait()


def geo_block(message, start):
    tiles = BLOCK // LANES
    return jnp.concatenate(
        [message[pl.ds(pl.multiple_of(start + t * GEO_ROWS, GEO_ROWS), GEO_ROWS), :] for t in range(tiles)],
        axis=1,
    )


def positions(geo):
    return (
        geo[6:7] + geo[7:8],
        geo[8:9] + geo[9:10],
        geo[10:11] + geo[11:12] + geo[12:13],
        geo[13:14] + geo[14:15],
    )


def make_columns(message, panel_rows, columns, features):
    per_block = BLOCK // LANES * GEO_ROWS
    for block in range(panel_rows // BLOCK):
        geo = geo_block(message, panel_rows + block * per_block).astype(F32)
        here_x, here_y, here_z, here_a = positions(geo)
        spots = jnp.concatenate([here_x, here_y, here_z, here_a, jnp.zeros((4, BLOCK), F32)], axis=0)
        columns[pl.ds(block * BLOCK, BLOCK), :] = spots.T
        high, low = halves((geo[0:3] + geo[3:6]) * BLOCK ** (-0.5))
        gap = jnp.zeros((10, BLOCK), F32)
        parts = [high, high, gap, low, low, gap]
        for piece in (0, 1):
            at_x, at_y, at_a = (geo[k + piece : k + piece + 1] for k in (6, 8, 13))
            hole = jnp.zeros((6, BLOCK), F32)
            parts += [hole, -2.0 * at_x, -2.0 * at_x, -2.0 * at_y, -2.0 * at_y, hole[0:3]]
            parts += [2.0 * at_a, 2.0 * at_a, hole[0:1]]
        parts += [jnp.ones((3, BLOCK), F32), thirds(here_x * here_x + here_y * here_y + here_a * here_a)]
        parts += [-2.0 * geo[6:10], jnp.zeros((6, BLOCK), F32)]
        features[pl.ds(block * BLOCK, BLOCK), :] = jnp.concatenate(parts, axis=0).T.astype(BF16)


def stage_kernel(offsets, sizes, early, role, *refs):
    message_rows, panel_rows = sizes
    count = len(offsets)
    source_count = 1 if role in ALONE else count
    sources, refs = refs[:source_count], refs[source_count:]
    if role == "first":
        columns, features, total = refs[:3]
        refs = refs[3:]
    else:
        own_info, columns, features, total_in, total = refs[:5]
        refs = refs[5:]
    counts, counts_s, items, tile_even, tile_odd, count_sem = refs[:6]
    toward_mate = 1 - 2 * lax.rem(lax.axis_index("gy"), 2)
    steps = [(jnp.int32(step_x), side * toward_mate) for step_x, side in offsets]

    copies = []
    if role in ALONE:
        message = sources[0]
        infos, info_starts = message, [index * message_rows + panel_rows for index in range(count)]
    else:
        message, infos, sems, info_sems = refs[6:]
        info_starts = [index * 32 for index in range(count)]
        info_copies = []
        for index, source in enumerate(sources):
            info_copies.append(
                pltpu.make_async_copy(
                    source.at[pl.ds(panel_rows, 32), :], infos.at[pl.ds(index * 32, 32), :], info_sems.at[index]
                )
            )
            copies.append(
                pltpu.make_async_copy(
                    source, message.at[pl.ds(index * message_rows, message_rows), :], sems.at[index]
                )
            )
        for copy in info_copies:
            copy.start()
        copies[0].start()
    if role == "first":
        total[...] = jnp.zeros_like(total)
    else:
        total[...] = total_in[...]
    tile_odd[...] = jnp.zeros_like(tile_odd)
    if role not in ALONE:
        for copy in info_copies:
            copy.wait()

    def info_of(ref, start):
        return ref[start : start + 16, :].astype(F32)[15:16], ref[start + 16 : start + 32, :].astype(F32)[15:16]

    lane = lax.broadcasted_iota(jnp.int32, (1, LANES), 1)
    own_first, own_second = info_of(infos if role == "first" else own_info, 0)
    codes = []
    for index, (step_x, step_y) in enumerate(steps):
        near = (step_x + 1) * 3 + step_y + 1
        far_first, far_second = info_of(infos, info_starts[index])
        own_block = own_second - (1 + 8 * near).astype(F32)
        far_block = far_second - (1 + 8 * (8 - near)).astype(F32)
        own_fits = (own_block >= 0.0) & (own_block < 8.0)
        far_fits = (far_block >= 0.0) & (far_block < 8.0)
        if offsets[index] == (0, 0):
            far_fits = far_fits & (far_block != far_first)
        own_code = jnp.where(own_fits, own_first * 8.0 + own_block, -1.0)
        far_code = jnp.where(far_fits, far_block * 8.0 + far_first, -1.0)
        codes.append(jnp.where(lane < CODES, own_code, far_code))
    row = lax.broadcasted_iota(jnp.int32, (CODES, LANES), 0).astype(F32)
    hits = jnp.concatenate([(row == code).astype(F32) for code in codes], axis=0).astype(BF16)
    counts[...] = lax.dot_general(
        jnp.ones((8, LANES), BF16), hits, (((1,), (1,)), ((), ())), preferred_element_type=F32
    ).astype(jnp.int32)
    count_copy = pltpu.make_async_copy(counts, counts_s, count_sem)
    count_copy.start()
    if role not in ALONE:
        copies[0].wait()
        for copy in copies[1:]:
            copy.start()
    if role == "first":
        make_columns(message, panel_rows, columns, features)
    count_copy.wait()

    def gather(code, used):
        often = counts_s[0, code]
        items[used] = code + often * 1024
        return used + jnp.minimum(often, 1)

    begin = jnp.int32(0)
    used = lax.fori_loop(0, early * CODES, gather, jnp.int32(0), unroll=8)
    if role == "first":
        used = jnp.minimum(used, EARLY)
    else:
        begin = jnp.minimum(used, EARLY)
        used = lax.fori_loop(early * CODES, count * CODES, gather, used, unroll=8)
    items[used] = 0
    items[used + 1] = 0

    def decode(item):
        code = item & 1023
        return code >> 6, (code >> 3) & 7, code & 7, (item >> 10).astype(F32)

    def build(item, tile):
        source, mine, block, _ = decode(item)
        first_row = pl.multiple_of(mine * BLOCK, BLOCK)
        geo = geo_block(
            message, source * message_rows + panel_rows + block * (BLOCK // LANES * GEO_ROWS)
        )
        near_x, near_y, near_z, near_a = positions(geo.astype(F32))
        step_x, step_y = steps[0]
        for index in range(1, count):
            step_x = jnp.where(source == index, steps[index][0], step_x)
            step_y = jnp.where(source == index, steps[index][1], step_y)
        step_x, step_y = step_x.astype(F32), step_y.astype(F32)
        near_x = near_x + step_x
        near_y = near_y + step_y
        extra = jnp.concatenate(
            [
                thirds(near_x * near_x + near_y * near_y + near_a * near_a),
                jnp.ones((3, BLOCK), F32),
                jnp.full((2, BLOCK), step_x),
                jnp.full((2, BLOCK), step_y),
                jnp.zeros((6, BLOCK), F32),
            ],
            axis=0,
        ).astype(BF16)
        for_aligned = jnp.concatenate([geo, geo, jnp.zeros((48, BLOCK), BF16)], axis=0)
        for_spread = jnp.concatenate([jnp.zeros((32, BLOCK), BF16), geo, geo, extra], axis=0)
        spots = columns[pl.ds(first_row, BLOCK), :]
        feature = features[pl.ds(first_row, BLOCK), :]
        for turn, start in enumerate(range(0, BLOCK, CHUNK)):
            spot = spots[start : start + CHUNK]
            aligned = jnp.dot(feature[start : start + CHUNK], for_aligned, preferred_element_type=F32)
            diff_z = spot[:, 2:3] - near_z
            if turn % 2 == 1:
                spread = jnp.dot(feature[start : start + CHUNK], for_spread, preferred_element_type=F32)
                spread = spread + diff_z * diff_z
            else:
                diff_x = spot[:, 0:1] - near_x
                diff_y = spot[:, 1:2] - near_y
                reach = spot[:, 3:4] + near_a
                spread = diff_x * diff_x + diff_y * diff_y + diff_z * diff_z + reach * reach
            tile[start : start + CHUNK, :] = (aligned * lax.rsqrt(spread)).astype(BF16)

    def apply(item, tile):
        source, mine, block, often = decode(item)
        near_panel = message[
            pl.ds(pl.multiple_of(source * message_rows + block * BLOCK, BLOCK), BLOCK), :
        ]
        product = jnp.dot(tile[...], near_panel, preferred_element_type=F32)
        span = pl.ds(pl.multiple_of(mine * BLOCK, BLOCK), BLOCK)
        total[span, :] += product * often

    def arrive(seen, needed):
        for index in range(1, len(copies)):
            @pl.when((seen < index) & (index <= needed))
            def _(index=index):
                copies[index].wait()

    def step(index, carry):
        last, seen = carry
        even, odd = items[begin + 2 * index], items[begin + 2 * index + 1]
        needed = jnp.maximum(jnp.maximum(decode(even)[0], decode(odd)[0]), seen)
        arrive(seen, needed)
        apply(last, tile_odd)
        build(even, tile_even)
        apply(even, tile_even)
        build(odd, tile_odd)
        return odd, needed

    last, seen = lax.fori_loop(0, (used - begin + 1) // 2, step, (jnp.int32(0), jnp.int32(0)))
    arrive(seen, jnp.int32(count - 1))
    apply(last, tile_odd)


def stage(role, offsets, early, sources, sizes, others):
    count = len(offsets)
    message_rows, panel_rows = sizes
    whole = pl.BlockSpec(memory_space=pltpu.VMEM)
    anywhere = pl.BlockSpec(memory_space=pl.ANY)
    out_shape, out_specs = jax.ShapeDtypeStruct((panel_rows, LANES), F32), whole
    if role == "first":
        out_shape = (
            jax.ShapeDtypeStruct((panel_rows, 8), F32),
            jax.ShapeDtypeStruct((panel_rows, 80), BF16),
            out_shape,
        )
        out_specs = (whole,) * 3
    scratch_shapes = [
        pltpu.VMEM((8, count * CODES), jnp.int32),
        pltpu.SMEM((8, count * CODES), jnp.int32),
        pltpu.SMEM((count * CODES + 2,), jnp.int32),
        pltpu.VMEM((BLOCK, BLOCK), BF16),
        pltpu.VMEM((BLOCK, BLOCK), BF16),
        pltpu.SemaphoreType.DMA,
    ]
    room = 12
    if role not in ALONE:
        room += 2 * count
        scratch_shapes += [
            pltpu.VMEM((count * message_rows, LANES), BF16),
            pltpu.VMEM((count * 32, LANES), BF16),
            pltpu.SemaphoreType.DMA((count,)),
            pltpu.SemaphoreType.DMA((count,)),
        ]
    return pl.pallas_call(
        functools.partial(stage_kernel, offsets, sizes, early, role),
        out_shape=out_shape,
        in_specs=[whole if role in ALONE else anywhere] * len(sources) + [whole] * len(others),
        out_specs=out_specs,
        scratch_shapes=scratch_shapes,
        input_output_aliases={} if role in ("first", "last") else {len(sources) + len(others) - 1: 0},
        compiler_params=pltpu.CompilerParams(vmem_limit_bytes=room * 2**20),
    )(*sources, *others)


def swapped(array, first):
    lower = range(first, lax.axis_size("gy") - 1, 2)
    pairs = [(i, i + 1) for i in lower] + [(i + 1, i) for i in lower]
    return lax.ppermute(array, "gy", pairs)


def shifted(array, axis, by):
    devices = lax.axis_size(axis)
    pairs = [(i, i + by) for i in range(devices) if 0 <= i + by < devices]
    return lax.ppermute(array, axis, pairs)


def shards(geometry, panel, pair_first, pair_second, pair_count):
    panel_rows = panel.shape[0]
    message_rows = panel_rows + geometry.shape[1] // LANES * GEO_ROWS
    slots = pair_first.shape[0]
    hbm = pl.BlockSpec(memory_space=pltpu.HBM)
    message = pl.pallas_call(
        pack_kernel,
        out_shape=jax.ShapeDtypeStruct((message_rows, LANES), BF16),
        in_specs=[pl.BlockSpec(memory_space=pltpu.SMEM), hbm, hbm, hbm, hbm],
        out_specs=pl.BlockSpec(memory_space=pltpu.VMEM),
        scratch_shapes=[
            pltpu.VMEM((1, slots), jnp.int32),
            pltpu.VMEM((1, slots), jnp.int32),
            pltpu.VMEM(geometry.shape, F32),
            pltpu.SemaphoreType.DMA((4,)),
        ],
        compiler_params=pltpu.CompilerParams(vmem_limit_bytes=62 * 2**20),
        name="pack",
    )(pair_count, pair_first.reshape(1, slots), pair_second.reshape(1, slots), geometry, panel)
    from_mate, from_far = swapped(message, 0), swapped(message, 1)
    from_left, from_right = shifted(message, "gx", 1), shifted(message, "gx", -1)
    sizes = (message_rows, panel_rows)
    columns, features, total = stage("first", ((0, 0), (0, 1)), 2, (message, from_mate), sizes, ())
    info = lax.slice_in_dim(message, panel_rows, panel_rows + 32, axis=0)
    from_left, from_right, total = lax.optimization_barrier((from_left, from_right, total))
    both = jnp.concatenate([from_left, from_right], axis=0)
    mate_corners, far_corners = swapped(both, 0), swapped(both, 1)
    total = stage(
        "second", ((0, 0), (0, 1), (0, -1), (-1, 0), (1, 0)), 2,
        (message, from_mate, from_far, from_left, from_right), sizes, (info, columns, features, total),
    )
    for role, side, corners in (("corner", 1, mate_corners), ("last", -1, far_corners)):
        total = stage(
            role, ((-1, side), (1, side)), 0, (corners,), sizes, (info, columns, features, total)
        )
    return total


def solution(mesh):
    in_specs = (
        P(None, ("gx", "gy")),
        P(("gx", "gy"), None),
        P(("gx", "gy")),
        P(("gx", "gy")),
        P(("gx", "gy")),
    )
    out_specs = P(("gx", "gy"), None)
    return jax.shard_map(shards, mesh=mesh, in_specs=in_specs, out_specs=out_specs, check_vma=False)
```
